256 devices in a mesh: expert: 16 (over x, y), context: 8 (over z_hi, core), dp: 2 (over z_lo).
Axes of the slice: x: 4, y: 4, z: 8 (z_hi: 4, z_lo: 2; z = z_hi * 2 + z_lo), core: 2. Of those that a mesh axis runs over, the one named last changes fastest.
Arguments:
- tokens: bfloat16 [32768, 2048], P(('expert', 'context', 'dp')), may hold values from -6 to 6
- routes: int32 [32768, 2], P(('expert', 'context', 'dp')), may hold values from 0 to 127, all different within a row; in each aligned block of 128 rows (0 to 127, 128 to 255, ...) at most 4 rows name the same one
- gates: float32 [32768, 2], P(('expert', 'context', 'dp')), may hold values from 0.3 to 0.9
- out_grad: bfloat16 [32768, 2048], P(('expert', 'context', 'dp')), may hold values from -6 to 6
- w_gate: bfloat16 [128, 2048, 768], P(('expert', 'context'), 'dp'), may hold values from -0.125 to 0.125
- w_up: bfloat16 [128, 2048, 768], P(('expert', 'context'), 'dp'), may hold values from -0.125 to 0.125
- w_down: bfloat16 [128, 2048, 768], P(('expert', 'context'), 'dp'), may hold values from -0.21875 to 0.21875
Outputs:
- mixed: bfloat16 [32768, 2048], P(('expert', 'context', 'dp'))
- token_grad: bfloat16 [32768, 2048], P(('expert', 'context', 'dp'))
- gate_grad: float32 [32768, 2], P(('expert', 'context', 'dp'))
- w_gate_grad: bfloat16 [128, 2048, 768], P(('expert', 'context'), 'dp')
- w_up_grad: bfloat16 [128, 2048, 768], P(('expert', 'context'), 'dp')
- w_down_grad: bfloat16 [128, 2048, 768], P(('expert', 'context'), 'dp')
The draws below stay inside these ranges and needn't reach their ends.
Inputs may be any that keep to these rules, and one draw needn't show every extreme that they name: `routes`: each row names 2 different experts; in each aligned block of 128 rows (the rows of one device) no expert is named by more than 4 rows, a bound that some block reaches.
All inputs are finite; a program needn't handle non-finite values.
Results may differ from the reference program's by a relative error of at most 0.0065.
Values may be sent and summed in bfloat16 or wider, within the bound.
A program may use at most 128 MiB of HBM per device.

```python
import math
import jax
import jax.numpy as jnp
import numpy as np
from jax import lax

D = 2048
FF = 768
TOP = 2
TOK_DEV = 128
EXPERTS = 128
CAP = 4
TOKENS = 32768
N_EXPERT = 16
N_CONTEXT = 8
N_DP = 2


def shard_levels(own_key, extent, cuts, least, top_value):
    factor_of, own = 1.0, jax.random.fold_in(own_key, 6)
    for position, parts in cuts:
        heights = jnp.exp(jax.random.uniform(jax.random.fold_in(own, position), (parts,), jnp.float32, least / len(cuts), top_value / len(cuts)))
        factor_of = factor_of * jnp.repeat(heights, extent[position] // parts).reshape([-1 if axis == position else 1 for axis in range(len(extent))])
    return factor_of


def shared_out(key, own, number, rows, number_of, top, reach, skew):
    sequence = jax.random.permutation(key, number_of)
    packed, usual = load_shares(number_of, rows * top, reach, skew, True), load_shares(number_of, rows * top, reach, skew, False)
    places = jnp.arange(number_of)

    def named(tallies, rotation):
        used = int((tallies > 0).sum())
        fixed = max(1, used // 4)
        passed = fixed + (places - fixed + rotation * (used - fixed)) % max(1, number_of - fixed)
        return jnp.zeros((number_of,), jnp.int32).at[sequence[jnp.where(places < fixed, places, passed)]].set(jnp.asarray(tallies, jnp.int32))

    tallies = jnp.where(number % 4 == 0, named(packed, number // 4), named(usual, number - number // 4 - 1))
    mixed = jax.random.permutation(jax.random.fold_in(own, 3), number_of)
    source_of, taker = mixed[0:number_of // 2 * 2:2], mixed[1:number_of // 2 * 2:2]
    margin = jnp.minimum(tallies[source_of] - 1, reach - tallies[taker]) // 2
    margin = jnp.where((source_of == sequence[0]) | (taker == sequence[0]) | (tallies[taker] == 0), 0, jnp.maximum(margin, 0))
    passed = jax.random.randint(jax.random.fold_in(own, 4), (number_of // 2,), 0, 1 << 20) % (margin + 1)
    tallies = tallies.at[source_of].add(-passed).at[taker].add(passed)
    items = jnp.searchsorted(jnp.cumsum(tallies), jnp.arange(rows * top), side="right").astype(jnp.int32)
    listing = items.reshape(top, rows).T
    listing = listing[jax.random.permutation(jax.random.fold_in(own, 1), rows)]
    rotation = jax.random.randint(jax.random.fold_in(own, 2), (rows, 1), 0, top)
    return jnp.take_along_axis(listing, (jnp.arange(top)[None, :] + rotation) % top, axis=1)


def load_shares(count, total, bound, skew, full):
    weights = [(1 << 20) // math.isqrt(grade ** skew) + 1 for grade in range(1, count + 1)]
    largest = bound if full else min(bound, max(-(-total // count), total * weights[0] // sum(weights)))
    least = 1 if total - largest >= count - 1 else 0
    counts, rest = [largest] + [least] * (count - 1), total - largest - least * (count - 1)
    while rest > 0:
        free = [i for i in range(1, count) if counts[i] < largest] or [i for i in range(1, count) if counts[i] < bound]
        pool, left = sum([weights[i] for i in free]), rest
        for i in free:
            more = min(bound - counts[i], max(1, left * weights[i] // pool), rest)
            counts[i] = counts[i] + more
            rest = rest - more
    return np.array(counts)


def normal_values(own_key, extent, deviation, reach, shards=(), kind=jnp.bfloat16):
    values = deviation * jax.random.normal(own_key, extent, jnp.float32)
    if shards:
        values = values * shard_levels(own_key, extent, shards, -0.22, 0.18)
    return jnp.clip(values, -reach, reach).astype(kind)


def setup_inputs(seed: int = 0) -> dict:
    streams_of = jax.random.split(jax.random.key(seed), 8)
    tokens = normal_values(streams_of[0], (TOKENS, D), 1.0, 6.0, ((0, 256),))
    routes_keys = jax.random.split(jax.random.fold_in(streams_of[1], 1), TOKENS // TOK_DEV)
    routes_turns = jax.random.permutation(jax.random.fold_in(streams_of[1], 3), TOKENS // TOK_DEV)
    routes = jax.vmap(lambda own, number: shared_out(jax.random.fold_in(streams_of[1], 2), own, number, TOK_DEV, EXPERTS, TOP, CAP, 2))(routes_keys, routes_turns).reshape((TOKENS, TOP))
    gates = jnp.clip(0.3 + 0.59999996 * jax.random.uniform(streams_of[2], (TOKENS, TOP), jnp.float32) ** shard_levels(streams_of[2], (TOKENS, TOP), ((0, 256),), -0.2, 0.2), 0.3, 0.9)
    out_grad = normal_values(streams_of[3], (TOKENS, D), 1.0, 6.0, ((0, 256),))
    w_gate = normal_values(streams_of[4], (EXPERTS, D, FF), D ** -0.5, 0.125, ((0, 128), (1, 2)))
    w_up = normal_values(streams_of[5], (EXPERTS, D, FF), D ** -0.5, 0.125, ((0, 128), (1, 2)))
    w_down = normal_values(streams_of[6], (EXPERTS, D, FF), FF ** -0.5, 0.21875, ((0, 128), (1, 2)))
    return {"tokens": tokens, "routes": routes, "gates": gates, "out_grad": out_grad, "w_gate": w_gate, "w_up": w_up, "w_down": w_down}


def contract(left, right, left_dim, right_dim):
    return lax.dot_general(left, right, (((left_dim,), (right_dim,)), ((), ())), preferred_element_type=jnp.float32)


def expert_block(rows_x, rows_dy, gate_w, up_w, down_w):
    gate_pre = contract(rows_x, gate_w, 1, 0)
    up_pre = contract(rows_x, up_w, 1, 0)
    sig_gate = jax.nn.sigmoid(gate_pre)
    active = gate_pre * sig_gate
    slope = sig_gate * (1.0 + gate_pre * (1.0 - sig_gate))
    hidden = (active * up_pre).astype(jnp.bfloat16)
    expert_out = contract(hidden, down_w, 1, 1).astype(jnp.bfloat16)
    hidden_grad = contract(rows_dy, down_w, 1, 0)
    grad_gate = (hidden_grad * up_pre * slope).astype(jnp.bfloat16)
    grad_up = (hidden_grad * active).astype(jnp.bfloat16)
    expert_dx = (contract(grad_gate, gate_w, 1, 1) + contract(grad_up, up_w, 1, 1)).astype(jnp.bfloat16)
    return expert_out, expert_dx, hidden, grad_gate, grad_up


def reference(tokens, routes, gates, out_grad, w_gate, w_up, w_down):
    most_rows = N_EXPERT * N_CONTEXT * N_DP * CAP
    slot_expert = routes.reshape(-1)
    gate_flat = gates.reshape(-1)

    def one_expert(carry, inputs):
        mixed_sum, token_sum, gate_sum = carry
        expert_id, gate_w, up_w, down_w = inputs
        chosen = slot_expert == expert_id
        slot_ids = jnp.nonzero(chosen, size=most_rows, fill_value=0)[0].astype(jnp.int32)
        live = jnp.arange(most_rows, dtype=jnp.int32) < jnp.sum(chosen.astype(jnp.int32))
        token_ids = (slot_ids // TOP).astype(jnp.int32)
        rows_x = jnp.where(live[:, None], tokens[token_ids], jnp.zeros((), tokens.dtype))
        cot_rows = jnp.where(live[:, None], out_grad[token_ids], jnp.zeros((), out_grad.dtype))
        gate_vals = jnp.where(live, gate_flat[slot_ids], jnp.zeros((), gates.dtype))
        rows_dy = (gate_vals[:, None] * cot_rows.astype(jnp.float32)).astype(jnp.bfloat16)
        expert_out, expert_dx, hidden, grad_gate, grad_up = expert_block(rows_x, rows_dy, gate_w, up_w, down_w)
        mixed_sum = mixed_sum.at[token_ids].add(gate_vals[:, None] * expert_out.astype(jnp.float32))
        token_sum = token_sum.at[token_ids].add(jnp.where(live[:, None], expert_dx.astype(jnp.float32), jnp.zeros((), jnp.float32)))
        products = jnp.sum(expert_out.astype(jnp.float32) * cot_rows.astype(jnp.float32), axis=1)
        gate_sum = gate_sum.at[slot_ids].add(jnp.where(live, products, jnp.zeros((), jnp.float32)))
        grads = (contract(rows_x, grad_gate, 0, 0).astype(jnp.bfloat16), contract(rows_x, grad_up, 0, 0).astype(jnp.bfloat16), contract(rows_dy, hidden, 0, 0).astype(jnp.bfloat16))
        return (mixed_sum, token_sum, gate_sum), grads

    start = (jnp.zeros((TOKENS, D), jnp.float32), jnp.zeros((TOKENS, D), jnp.float32), jnp.zeros((TOKENS * TOP,), jnp.float32))
    carry, grads = lax.scan(one_expert, start, (jnp.arange(EXPERTS, dtype=jnp.int32), w_gate, w_up, w_down))
    mixed = carry[0].astype(jnp.bfloat16)
    token_grad = carry[1].astype(jnp.bfloat16)
    gate_grad = carry[2].reshape(TOKENS, TOP)
    return (mixed, token_grad, gate_grad, grads[0], grads[1], grads[2])
```

```python
import jax
import jax.numpy as jnp
from jax import lax
from jax.sharding import PartitionSpec as P

PEERS = ("dp", "expert", "context")


def contract(left, right, left_dim, right_dim):
    return lax.dot_general(
        left, right, (((left_dim,), (right_dim,)), ((), ())), preferred_element_type=jnp.float32
    )


def shards(tokens, routes, gates, out_grad, w_gate, w_up, w_down):
    experts = lax.axis_size(("expert", "context"))
    halves = lax.axis_size("dp")
    devices = experts * halves
    local_tokens, top_count = routes.shape
    width = tokens.shape[1] // halves
    ff = w_gate.shape[2]
    capacity = max(2, 2 * local_tokens * top_count // experts)
    block = 2 * capacity

    slots = jnp.concatenate([routes[:, k] for k in range(top_count)])
    count = slots.shape[0]
    order = lax.broadcasted_iota(jnp.int32, (count, count), 0)
    before = lax.broadcasted_iota(jnp.int32, (count, count), 1) < order
    place = jnp.sum(((slots[:, None] == slots[None, :]) & before).astype(jnp.int32), axis=1)
    place = (slots * block + place).reshape(top_count, local_tokens)
    rows = lax.broadcasted_iota(jnp.int32, (experts * block, local_tokens), 0)
    hits_x = [rows == place[k][None, :] for k in range(top_count)]
    hits_dy = [rows == place[k][None, :] + capacity for k in range(top_count)]
    pick_x = sum(h.astype(jnp.bfloat16) for h in hits_x)
    pick_dy = sum(h.astype(jnp.bfloat16) for h in hits_dy)
    gate_of = sum(
        jnp.sum(jnp.where(h, gates[:, k][None, :], 0.0), axis=1) for k, h in enumerate(hits_dy)
    )

    def half(array, h):
        return array[:, h * width : (h + 1) * width]

    sends = []
    for h in range(halves):
        picked = contract(pick_x, half(tokens, h), 1, 0)
        graded = gate_of[:, None] * contract(pick_dy, half(out_grad, h), 1, 0)
        sends.append((picked + graded).astype(jnp.bfloat16))
    send = jnp.stack(sends).reshape(devices, block, width)
    recv = lax.all_to_all(send, PEERS, split_axis=0, concat_axis=0, tiled=True)
    rows_x = recv[:, :capacity].reshape(devices * capacity, width)
    rows_dy = recv[:, capacity:].reshape(devices * capacity, width)

    gate_w, up_w, down_w = w_gate[0], w_up[0], w_down[0]
    part_gate = contract(rows_x, gate_w, 1, 0)
    part_up = contract(rows_x, up_w, 1, 0)
    part_hidden = contract(rows_dy, down_w, 1, 0)
    swap = [(d, halves - 1 - d) for d in range(halves)]
    mine = jnp.concatenate(
        [p.astype(jnp.bfloat16) for p in (part_gate, part_up, part_hidden)], axis=1
    )
    other = lax.ppermute(mine, "dp", swap).astype(jnp.float32)
    gate_pre = part_gate + other[:, :ff]
    up_pre = part_up + other[:, ff : 2 * ff]
    hidden_grad = part_hidden + other[:, 2 * ff :]
    sig_gate = jax.nn.sigmoid(gate_pre)
    active = gate_pre * sig_gate
    slope = sig_gate * (1.0 + gate_pre * (1.0 - sig_gate))
    hidden = (active * up_pre).astype(jnp.bfloat16)
    grad_gate = (hidden_grad * up_pre * slope).astype(jnp.bfloat16)
    grad_up = (hidden_grad * active).astype(jnp.bfloat16)
    expert_out = contract(hidden, down_w, 1, 1).astype(jnp.bfloat16)
    expert_dx = (contract(grad_gate, gate_w, 1, 1) + contract(grad_up, up_w, 1, 1)).astype(
        jnp.bfloat16
    )
    back = jnp.concatenate(
        [
            expert_out.reshape(devices, capacity, width),
            expert_dx.reshape(devices, capacity, width),
        ],
        axis=1,
    )
    back = lax.all_to_all(back, PEERS, split_axis=0, concat_axis=0, tiled=True)
    back = back.reshape(halves, experts * block, width)
    mixed, token_grad, gate_grad = [], [], 0.0
    for h in range(halves):
        outs = [contract(x.astype(jnp.bfloat16), back[h], 0, 0) for x in hits_x]
        cot = half(out_grad, h).astype(jnp.float32)
        mixed.append(sum(gates[:, k][:, None] * out for k, out in enumerate(outs)))
        gate_grad += jnp.stack([jnp.sum(out * cot, axis=1) for out in outs], axis=1)
        token_grad.append(contract(pick_dy, back[h], 0, 0))
    mixed = jnp.concatenate(mixed, axis=1).astype(jnp.bfloat16)
    token_grad = jnp.concatenate(token_grad, axis=1).astype(jnp.bfloat16)
    w_gate_grad = contract(rows_x, grad_gate, 0, 0).astype(jnp.bfloat16)[None]
    w_up_grad = contract(rows_x, grad_up, 0, 0).astype(jnp.bfloat16)[None]
    w_down_grad = contract(rows_dy, hidden, 0, 0).astype(jnp.bfloat16)[None]
    return (mixed, token_grad, gate_grad, w_gate_grad, w_up_grad, w_down_grad)


def solution(mesh):
    by_token = P(("expert", "context", "dp"), None)
    by_expert = P(("expert", "context"), "dp", None)
    return jax.shard_map(
        shards,
        mesh=mesh,
        in_specs=(by_token,) * 4 + (by_expert,) * 3,
        out_specs=(by_token,) * 3 + (by_expert,) * 3,
        check_vma=False,
    )
```

```python
import functools

import jax
import jax.numpy as jnp
from jax import lax
from jax.experimental import pallas as pl
from jax.experimental.pallas import tpu as pltpu
from jax.sharding import PartitionSpec as P

MESH = pl.DeviceIdType.MESH
X, Y, Z = 4, 4, 8
PLANE = X * Y * 2
ROWS = 8 * PLANE


def contract(left, right, left_dim, right_dim):
    return lax.dot_general(
        left, right, (((left_dim,), (right_dim,)), ((), ())), preferred_element_type=jnp.float32
    )


def plane_order(z, g):
    pair = (z // 2 + (g // 2 % 2) * 2 + g // 4) % (Z // 2)
    return pair * 2 + g % 2


def experts_kernel(
    send_ref, gate_ref, up_ref, down_ref, back_ref, gate_out, up_out, down_out,
    recv, relay, own_a, own_b, mine, other, ret, relay_back, terms,
    recv_sem, send_sem, relay_sem, forward_sem, mine_sem, other_sem,
    ret_sem, relay_back_sem, forward_back_sem, back_sem,
):
    expert, context, z_lo = (lax.axis_index(a) for a in ("expert", "context", "dp"))
    x, y, core = expert // Y, expert % Y, context % 2
    z = context // 2 * 2 + z_lo
    ff = gate_ref.shape[1]
    half = ff // 2

    def device(x, y, z, core):
        return (x * Y + y, z // 2 * 2 + core, z % 2)

    def place(x, y, z, core):
        return z % 2 * 128 + (x * Y + y) * 8 + z // 2 * 2 + core

    def peer(j):
        return (x + j % X) % X, (y + j // X % Y) % Y, (core + j // (X * Y)) % 2

    me = place(x, y, z, core)
    my_slot = z * PLANE + expert * 2 + core

    barrier = pltpu.get_barrier_semaphore()

    def greet(i, _):
        g, j = i // PLANE, i % PLANE
        px, py, pc = peer(j)
        to = device(px, py, (z + g) % Z, pc)
        pl.semaphore_signal(barrier, inc=1, device_id=to, device_id_type=MESH)
        return 0

    lax.fori_loop(1, Z * PLANE, greet, 0)
    pl.semaphore_wait(barrier, Z * PLANE - 1)

    def push(src, dst, sent, arrived, to):
        pltpu.make_async_remote_copy(
            src_ref=src, dst_ref=dst, send_sem=sent, recv_sem=arrived, device_id=to, device_id_type=MESH
        ).start()

    opposite = (z + Z // 2) % Z
    before, beyond = (z + Z - 1) % Z, (z + 1) % Z

    def by_relay(block, relay_to, sent, arrived):
        def one(j, _):
            px, py = (x + j % X) % X, (y + j // X) % Y
            push(block(px, py, opposite, 1), relay_to.at[px * Y + py], sent, arrived,
                 device(x, y, before, core))
            return 0

        lax.fori_loop(0, X * Y, one, 0)

    def forward(relay_from, dst, sent, arrived):
        def one(j, _):
            px, py = (x + j % X) % X, (y + j // X) % Y
            push(relay_from.at[px * Y + py], dst, sent, arrived,
                 device(px, py, (beyond + Z // 2) % Z, 1))
            return 0

        lax.fori_loop(0, X * Y, one, 0)

    def to_plane(plane, block, dst, sent, arrived):
        def one(j, _):
            px, py, pc = peer(j)

            @pl.when((plane != z) | (j > 0))
            def _():
                @pl.when((plane != opposite) | (pc == 0))
                def _():
                    push(block(px, py, plane, pc), dst, sent, arrived, device(px, py, plane, pc))

            return 0

        lax.fori_loop(0, PLANE, one, 0)

    def wait(ref, sem):
        pltpu.make_async_copy(ref, ref, sem).wait()

    def out_block(px, py, pz, pc):
        return send_ref.at[place(px, py, pz, pc)]

    by_relay(out_block, relay, send_sem, relay_sem)
    pltpu.make_async_copy(send_ref.at[me], recv.at[my_slot], recv_sem.at[z]).start()

    def dispatch(g, _):
        to_plane(plane_order(z, g), out_block, recv.at[my_slot], send_sem, recv_sem.at[z])
        return 0

    lax.fori_loop(0, 4, dispatch, 0)
    wait(relay, relay_sem)
    forward(relay, recv.at[beyond * PLANE + expert * 2 + core], forward_sem, recv_sem.at[beyond])
    lax.fori_loop(4, Z, dispatch, 0)

    token_row = lax.broadcasted_iota(jnp.int32, (ROWS, half), 0) % 8 < 4

    def rows_of(value):
        return value.astype(jnp.float32).reshape(-1, value.shape[-1])

    def partial_sums(g, _):
        plane = plane_order(z, g)
        here = pl.ds(pl.multiple_of(plane * PLANE, PLANE), PLANE)
        wait(recv.at[here], recv_sem.at[plane])
        rows = rows_of(recv[here]).astype(jnp.bfloat16)
        for h in range(2):
            cols = slice(h * half, (h + 1) * half)
            part = jnp.where(
                token_row,
                contract(rows, gate_ref[:, cols], 1, 0),
                contract(rows, down_ref[:, cols], 1, 0),
            )
            own_a[plane, :, cols] = part
            mine[plane, :, cols] = part.astype(jnp.bfloat16)
        part = jnp.where(
            token_row,
            contract(rows, up_ref[:, :half], 1, 0),
            pltpu.roll(contract(rows, up_ref[:, half:], 1, 0), 4, 0),
        )
        own_b[plane] = part
        mine[plane, :, ff:] = part.astype(jnp.bfloat16)
        push(mine.at[plane], other.at[plane], mine_sem, other_sem.at[plane],
             (expert, context, 1 - z_lo))
        return 0

    lax.fori_loop(0, Z, partial_sums, 0)

    def back_block(px, py, pz, pc):
        return ret.at[pz * PLANE + (px * Y + py) * 2 + pc]

    def finish(g, _):
        plane = plane_order(z, g)
        wait(other.at[plane], other_sem.at[plane])
        up_two = own_b[plane] + other[plane, :, ff:].astype(jnp.float32)
        total = jnp.zeros((ROWS, gate_ref.shape[0]), jnp.float32)
        at = pl.ds(pl.multiple_of(plane * ROWS, ROWS), ROWS)
        for h in range(2):
            cols = slice(h * half, (h + 1) * half)
            both = own_a[plane, :, cols] + other[plane, :, cols].astype(jnp.float32)
            gate_pre = jnp.where(token_row, both, pltpu.roll(both, 4, 0))
            if h == 0:
                up_pre = jnp.where(token_row, up_two, pltpu.roll(up_two, 4, 0))
            else:
                up_pre = jnp.where(token_row, pltpu.roll(up_two, ROWS - 4, 0), up_two)
            sig_gate = jax.nn.sigmoid(gate_pre)
            active = gate_pre * sig_gate
            slope = sig_gate * (1.0 + gate_pre * (1.0 - sig_gate))
            hidden = jnp.where(token_row, active * up_pre, 0.0)
            grad_gate = jnp.where(token_row, 0.0, both * up_pre * slope)
            grad_up = jnp.where(token_row, 0.0, both * active)
            total += contract(hidden.astype(jnp.bfloat16), down_ref[:, cols], 1, 1)
            total += contract(grad_gate.astype(jnp.bfloat16), gate_ref[:, cols], 1, 1)
            total += contract(grad_up.astype(jnp.bfloat16), up_ref[:, cols], 1, 1)
            terms[at, h * half : (h + 1) * half] = pltpu.roll(grad_gate, ROWS - 4, 0).astype(
                jnp.bfloat16
            )
            terms[at, ff + h * half : ff + (h + 1) * half] = pltpu.roll(
                grad_up, ROWS - 4, 0
            ).astype(jnp.bfloat16)
            terms[at, 2 * ff + h * half : 2 * ff + (h + 1) * half] = pltpu.roll(
                hidden, 4, 0
            ).astype(jnp.bfloat16)
        here = pl.ds(pl.multiple_of(plane * PLANE, PLANE), PLANE)
        ret[here] = total.reshape(PLANE, 8, total.shape[-1]).astype(jnp.bfloat16)

        @pl.when(plane == z)
        def _():
            pltpu.make_async_copy(ret.at[my_slot], back_ref.at[me], back_sem).start()

        @pl.when(plane == opposite)
        def _():
            by_relay(back_block, relay_back, ret_sem, relay_back_sem)

        to_plane(plane, back_block, back_ref.at[me], ret_sem, back_sem)
        return 0

    lax.fori_loop(0, 6, finish, 0)
    wait(relay_back, relay_back_sem)
    forward(relay_back, back_ref.at[place(x, y, beyond, core)], forward_back_sem, back_sem)
    lax.fori_loop(6, Z, finish, 0)

    step = 256

    def weight_grads(i, _):
        cols = pl.ds(pl.multiple_of(i * step, step), step)
        rows = rows_of(recv[:, :, cols]).T.astype(jnp.bfloat16)
        for n, out in enumerate((gate_out, up_out, down_out)):
            out[cols, :] = contract(rows, terms[:, n * ff : (n + 1) * ff], 1, 0).astype(jnp.bfloat16)
        return 0

    lax.fori_loop(0, gate_ref.shape[0] // step, weight_grads, 0)

    wait(recv.at[pl.ds(0, Z * PLANE - 1)], send_sem)
    wait(relay, forward_sem)
    wait(mine, mine_sem)
    wait(ret.at[pl.ds(0, Z * PLANE - 1)], ret_sem)
    wait(relay_back, forward_back_sem)
    wait(back_ref, back_sem)


def through_experts(send, gate_w, up_w, down_w):
    width, ff = gate_w.shape
    vmem = pl.BlockSpec(memory_space=pltpu.VMEM)
    hbm = pl.BlockSpec(memory_space=pl.ANY)
    bf16, f32, dma = jnp.bfloat16, jnp.float32, pltpu.SemaphoreType.DMA
    weight = jax.ShapeDtypeStruct((width, ff), bf16)
    return pl.pallas_call(
        experts_kernel,
        out_shape=(jax.ShapeDtypeStruct(send.shape, bf16), weight, weight, weight),
        in_specs=[hbm, vmem, vmem, vmem],
        out_specs=(hbm, vmem, vmem, vmem),
        scratch_shapes=[
            pltpu.VMEM(send.shape, bf16),
            pltpu.VMEM((X * Y,) + send.shape[1:], bf16),
            pltpu.VMEM((Z, ROWS, ff), f32),
            pltpu.VMEM((Z, ROWS, ff // 2), f32),
            pltpu.VMEM((Z, ROWS, ff + ff // 2), bf16),
            pltpu.VMEM((Z, ROWS, ff + ff // 2), bf16),
            pltpu.VMEM(send.shape, bf16),
            pltpu.VMEM((X * Y,) + send.shape[1:], bf16),
            pltpu.VMEM((Z * ROWS, 3 * ff), bf16),
            dma((Z,)), dma, dma, dma, dma, dma((Z,)), dma, dma, dma, dma,
        ],
        compiler_params=pltpu.CompilerParams(
            collective_id=0, has_side_effects=True, vmem_limit_bytes=63_000_000
        ),
    )(send, gate_w, up_w, down_w)


def shards(tokens, routes, gates, out_grad, w_gate, w_up, w_down):
    experts = lax.axis_size(("expert", "context"))
    halves = lax.axis_size("dp")
    devices = experts * halves
    local_tokens, top_count = routes.shape
    width = tokens.shape[1] // halves
    capacity = max(2, 2 * local_tokens * top_count // experts)
    block = 2 * capacity

    slots = jnp.concatenate([routes[:, k] for k in range(top_count)])
    count = slots.shape[0]
    order = lax.broadcasted_iota(jnp.int32, (count, count), 0)
    before = lax.broadcasted_iota(jnp.int32, (count, count), 1) < order
    place = jnp.sum(((slots[:, None] == slots[None, :]) & before).astype(jnp.int32), axis=1)
    place = (slots * block + place).reshape(top_count, local_tokens)
    rows = lax.broadcasted_iota(jnp.int32, (experts * block, local_tokens), 0)
    hits_x = [rows == place[k][None, :] for k in range(top_count)]
    hits_dy = [rows == place[k][None, :] + capacity for k in range(top_count)]
    pick_x = sum(h.astype(jnp.bfloat16) for h in hits_x)
    pick_dy = sum(h.astype(jnp.bfloat16) for h in hits_dy)
    gate_of = sum(
        jnp.sum(jnp.where(h, gates[:, k][None, :], 0.0), axis=1) for k, h in enumerate(hits_dy)
    )

    def half(array, h):
        return array[:, h * width : (h + 1) * width]

    sends = []
    for h in range(halves):
        picked = contract(pick_x, half(tokens, h), 1, 0)
        graded = gate_of[:, None] * contract(pick_dy, half(out_grad, h), 1, 0)
        sends.append((picked + graded).astype(jnp.bfloat16))
    send = jnp.stack(sends).reshape(devices, block, width)
    back, w_gate_grad, w_up_grad, w_down_grad = through_experts(
        send, w_gate[0], w_up[0], w_down[0]
    )
    back = back.reshape(halves, experts * block, width)
    mixed, token_grad, gate_grad = [], [], 0.0
    for h in range(halves):
        outs = [contract(x.astype(jnp.bfloat16), back[h], 0, 0) for x in hits_x]
        cot = half(out_grad, h).astype(jnp.float32)
        mixed.append(sum(gates[:, k][:, None] * out for k, out in enumerate(outs)))
        gate_grad += jnp.stack([jnp.sum(out * cot, axis=1) for out in outs], axis=1)
        token_grad.append(contract(pick_dy, back[h], 0, 0))
    mixed = jnp.concatenate(mixed, axis=1).astype(jnp.bfloat16)
    token_grad = jnp.concatenate(token_grad, axis=1).astype(jnp.bfloat16)
    return (mixed, token_grad, gate_grad, w_gate_grad[None], w_up_grad[None], w_down_grad[None])


def solution(mesh):
    by_token = P(("expert", "context", "dp"), None)
    by_expert = P(("expert", "context"), "dp", None)
    return jax.shard_map(
        shards,
        mesh=mesh,
        in_specs=(by_token,) * 4 + (by_expert,) * 3,
        out_specs=(by_token,) * 3 + (by_expert,) * 3,
        check_vma=False,
    )
```

```python
import jax
import jax.numpy as jnp
from jax import lax
from jax.experimental import pallas as pl
from jax.experimental.pallas import tpu as pltpu
from jax.sharding import PartitionSpec as P

MESH = pl.DeviceIdType.MESH
X, Y, Z = 4, 4, 8
PLANE = X * Y * 2
ROWS = 8 * PLANE


def contract(left, right, left_dim, right_dim):
    return lax.dot_general(
        left, right, (((left_dim,), (right_dim,)), ((), ())), preferred_element_type=jnp.float32
    )


def plane_order(z, g):
    pair = (z // 2 + (g // 2 % 2) * 2 + g // 4) % (Z // 2)
    return pair * 2 + g % 2


def return_order(z, g):
    pair = (z // 2 + (g // 2 % 2) * 2 + g // 4 * 3) % (Z // 2)
    return pair * 2 + g % 2


def places(one, other_way, axis):
    token = lax.broadcasted_iota(jnp.int32, (one[0].size, one[0].size), axis)
    earlier = token < lax.broadcasted_iota(jnp.int32, token.shape, 1 - axis)
    found = []
    for k, expert in enumerate(one):
        place = 0
        for n in range(k + 1):
            same = other_way[n] == expert
            same = same & earlier if n == k else same
            place += jnp.sum(same.astype(jnp.int32), axis=axis, keepdims=True)
        block = (expert // 2 % 4) * (2 * X * Y) * 2 + expert // 8 * 2 + expert % 2
        found.append(block * 8 + place)
    return found


def experts_kernel(
    tokens_ref, grad_ref, routes_ref, routes_t_ref, gates_ref, gates_t_ref, gate_ref, up_ref, down_ref,
    mixed_out, token_out, grad_out, gate_out, up_out, down_out,
    recv, own_a, own_b, mine, other, send, back, terms, sum_0, sum_1, sum_dx,
    recv_sem, self_sem, send_sem, mine_sem, other_sem, ret_sem, back_sem,
):
    expert, context, z_lo = (lax.axis_index(a) for a in ("expert", "context", "dp"))
    x, y, core = expert // Y, expert % Y, context % 2
    z = context // 2 * 2 + z_lo
    width, ff = gate_ref.shape
    half = ff // 2

    def device(x, y, z, core):
        return (x * Y + y, z // 2 * 2 + core, z % 2)

    def peer(j):
        return (x + j % X) % X, (y + j // X % Y) % Y, (core + j // (X * Y)) % 2

    my_slot = z * PLANE + expert * 2 + core

    barrier = pltpu.get_barrier_semaphore()

    def greet(i, _):
        g, j = i // PLANE, i % PLANE
        px, py, pc = peer(j)
        to = device(px, py, (z + g) % Z, pc)
        pl.semaphore_signal(barrier, inc=1, device_id=to, device_id_type=MESH)
        return 0

    lax.fori_loop(1, Z * PLANE, greet, 0)

    routes_col = [routes_ref[:, k : k + 1] for k in range(2)]
    routes_row = [routes_t_ref[k : k + 1, :] for k in range(2)]
    place_row = places(routes_row, routes_col, 0)
    place_col = places(routes_col, routes_row, 1)
    gates_row = [gates_t_ref[k : k + 1, :] for k in range(2)]
    tokens_here = tokens_ref.shape[0]
    sum_0[...] = jnp.zeros_like(sum_0)
    sum_1[...] = jnp.zeros_like(sum_1)
    sum_dx[...] = jnp.zeros_like(sum_dx)

    pl.semaphore_wait(barrier, Z * PLANE - 1)

    def push(src, dst, sent, arrived, to):
        pltpu.make_async_remote_copy(
            src_ref=src, dst_ref=dst, send_sem=sent, recv_sem=arrived, device_id=to, device_id_type=MESH
        ).start()

    def to_plane(plane, dst, sent, arrived):
        def one(j, _):
            px, py, pc = peer(j)

            @pl.when((plane != z) | (j > 0))
            def _():
                src = send.at[plane * PLANE + (px * Y + py) * 2 + pc]
                push(src, dst, sent, arrived, device(px, py, plane, pc))

            return 0

        lax.fori_loop(0, PLANE, one, 0)

    def wait(ref, sem):
        pltpu.make_async_copy(ref, ref, sem).wait()

    def blocks_of(plane):
        return pl.ds(pl.multiple_of(plane * PLANE, PLANE), PLANE)

    def columns_of(plane):
        return pl.ds(pl.multiple_of(plane % 2 * width, width), width)

    def rows_of(value):
        return value.astype(jnp.float32).reshape(-1, value.shape[-1])

    def dispatch(g, _):
        plane = plane_order(z, g)
        first = plane // 2 * (2 * ROWS)
        row = lax.broadcasted_iota(jnp.int32, (ROWS, tokens_here), 0) + first
        hits = [row == place for place in place_row]
        hits_dy = [row == place + 4 for place in place_row]
        pick = sum(h.astype(jnp.float32) for h in hits).astype(jnp.bfloat16)
        pick_dy = sum(h.astype(jnp.float32) for h in hits_dy).astype(jnp.bfloat16)
        gate_of = sum(
            jnp.sum(jnp.where(h, gate, 0.0), axis=1, keepdims=True)
            for h, gate in zip(hits_dy, gates_row, strict=True)
        )
        cols = columns_of(plane)
        block = contract(pick, tokens_ref[:, cols], 1, 0)
        block += gate_of * contract(pick_dy, grad_ref[:, cols], 1, 0)
        send[blocks_of(plane)] = block.reshape(PLANE, 8, width).astype(jnp.bfloat16)

        @pl.when(plane == z)
        def _():
            pltpu.make_async_copy(send.at[my_slot], recv.at[my_slot], self_sem).start()

        to_plane(plane, recv.at[my_slot], send_sem, recv_sem.at[z])
        return 0

    lax.fori_loop(0, Z, dispatch, 0)

    token_row = lax.broadcasted_iota(jnp.int32, (ROWS, half), 0) % 8 < 4

    def wait_plane(buffer, plane, sem):
        @pl.when(plane == z)
        def _():
            wait(buffer.at[my_slot], self_sem)
            wait(buffer.at[pl.ds(0, PLANE - 1)], sem.at[plane])

        @pl.when(plane != z)
        def _():
            wait(buffer.at[pl.ds(0, PLANE)], sem.at[plane])

    def partial_sums(g, _):
        plane = plane_order(z, g)
        wait_plane(recv, plane, recv_sem)
        rows = rows_of(recv[blocks_of(plane)]).astype(jnp.bfloat16)
        for h in range(2):
            cols = slice(h * half, (h + 1) * half)
            part = jnp.where(
                token_row,
                contract(rows, gate_ref[:, cols], 1, 0),
                contract(rows, down_ref[:, cols], 1, 0),
            )
            own_a[plane, :, cols] = part
            mine[plane, :, cols] = part.astype(jnp.bfloat16)
        part = jnp.where(
            token_row,
            contract(rows, up_ref[:, :half], 1, 0),
            pltpu.roll(contract(rows, up_ref[:, half:], 1, 0), 4, 0),
        )
        own_b[plane] = part
        mine[plane, :, ff:] = part.astype(jnp.bfloat16)
        push(mine.at[plane], other.at[plane], mine_sem, other_sem.at[plane],
             (expert, context, 1 - z_lo))
        return 0

    lax.fori_loop(0, Z, partial_sums, 0)
    wait(send.at[pl.ds(0, Z * PLANE - 1)], send_sem)

    def finish(g, _):
        plane = plane_order(z, g)
        wait(other.at[plane], other_sem.at[plane])
        up_two = own_b[plane] + other[plane, :, ff:].astype(jnp.float32)
        total = jnp.zeros((ROWS, width), jnp.float32)
        at = pl.ds(pl.multiple_of(plane * ROWS, ROWS), ROWS)
        for h in range(2):
            cols = slice(h * half, (h + 1) * half)
            both = own_a[plane, :, cols] + other[plane, :, cols].astype(jnp.float32)
            gate_pre = jnp.where(token_row, both, pltpu.roll(both, 4, 0))
            if h == 0:
                up_pre = jnp.where(token_row, up_two, pltpu.roll(up_two, 4, 0))
            else:
                up_pre = jnp.where(token_row, pltpu.roll(up_two, ROWS - 4, 0), up_two)
            sig_gate = jax.nn.sigmoid(gate_pre)
            active = gate_pre * sig_gate
            slope = sig_gate * (1.0 + gate_pre * (1.0 - sig_gate))
            hidden = jnp.where(token_row, active * up_pre, 0.0)
            grad_gate = jnp.where(token_row, 0.0, both * up_pre * slope)
            grad_up = jnp.where(token_row, 0.0, both * active)
            total += contract(hidden.astype(jnp.bfloat16), down_ref[:, cols], 1, 1)
            total += contract(grad_gate.astype(jnp.bfloat16), gate_ref[:, cols], 1, 1)
            total += contract(grad_up.astype(jnp.bfloat16), up_ref[:, cols], 1, 1)
            for n, (term, shift) in enumerate(
                ((grad_gate, ROWS - 4), (grad_up, ROWS - 4), (hidden, 4))
            ):
                terms[at, n * ff + h * half : n * ff + (h + 1) * half] = pltpu.roll(
                    term, shift, 0
                ).astype(jnp.bfloat16)
        send[blocks_of(plane)] = total.reshape(PLANE, 8, width).astype(jnp.bfloat16)

        @pl.when(plane == z)
        def _():
            pltpu.make_async_copy(send.at[my_slot], back.at[my_slot], self_sem).start()

        to_plane(plane, back.at[my_slot], ret_sem, back_sem.at[z])
        return 0

    lax.fori_loop(0, Z, finish, 0)

    step = 256

    def weight_grads(i, _):
        cols = pl.ds(pl.multiple_of(i * step, step), step)
        rows = rows_of(recv[:, :, cols]).T.astype(jnp.bfloat16)
        for n, out in enumerate((gate_out, up_out, down_out)):
            out[cols, :] = contract(rows, terms[:, n * ff : (n + 1) * ff], 1, 0).astype(jnp.bfloat16)
        return 0

    lax.fori_loop(0, width // step, weight_grads, 0)

    def combine(g, _):
        plane = return_order(z, g)
        wait_plane(back, plane, back_sem)
        rows = rows_of(back[blocks_of(plane)]).astype(jnp.bfloat16)
        first = plane // 2 * (2 * ROWS)
        col = lax.broadcasted_iota(jnp.int32, (tokens_here, ROWS), 1) + first
        hits = [(col == place).astype(jnp.float32) for place in place_col]
        hits.append(sum((col == place + 4).astype(jnp.float32) for place in place_col))
        cols = columns_of(plane)
        for hit, into in zip(hits, (sum_0, sum_1, sum_dx), strict=True):
            into[:, cols] += contract(hit.astype(jnp.bfloat16), rows, 1, 0)
        return 0

    lax.fori_loop(0, Z, combine, 0)
    out_grad = grad_ref[...].astype(jnp.float32)
    mixed_out[...] = (
        gates_ref[:, 0:1] * sum_0[...] + gates_ref[:, 1:2] * sum_1[...]
    ).astype(jnp.bfloat16)
    token_out[...] = sum_dx[...].astype(jnp.bfloat16)
    grad_out[:, 0:1] = jnp.sum(sum_0[...] * out_grad, axis=1, keepdims=True)
    grad_out[:, 1:2] = jnp.sum(sum_1[...] * out_grad, axis=1, keepdims=True)

    wait(mine, mine_sem)
    wait(send.at[pl.ds(0, Z * PLANE - 1)], ret_sem)


def shards(tokens, routes, gates, out_grad, w_gate, w_up, w_down):
    _, width, ff = w_gate.shape
    bf16, f32, dma = jnp.bfloat16, jnp.float32, pltpu.SemaphoreType.DMA
    blocks = (Z * PLANE, 8, width)
    weight = jax.ShapeDtypeStruct((width, ff), bf16)
    mixed, token_grad, gate_grad, w_gate_grad, w_up_grad, w_down_grad = pl.pallas_call(
        experts_kernel,
        out_shape=(
            jax.ShapeDtypeStruct(tokens.shape, bf16),
            jax.ShapeDtypeStruct(tokens.shape, bf16),
            jax.ShapeDtypeStruct(gates.shape, f32),
            weight, weight, weight,
        ),
        in_specs=[pl.BlockSpec(memory_space=pltpu.VMEM)] * 9,
        out_specs=(pl.BlockSpec(memory_space=pltpu.VMEM),) * 6,
        scratch_shapes=[
            pltpu.VMEM(blocks, bf16),
            pltpu.VMEM((Z, ROWS, ff), f32),
            pltpu.VMEM((Z, ROWS, ff // 2), f32),
            pltpu.VMEM((Z, ROWS, ff + ff // 2), bf16),
            pltpu.VMEM((Z, ROWS, ff + ff // 2), bf16),
            pltpu.VMEM(blocks, bf16),
            pltpu.VMEM(blocks, bf16),
            pltpu.VMEM((Z * ROWS, 3 * ff), bf16),
            pltpu.VMEM(tokens.shape, f32),
            pltpu.VMEM(tokens.shape, f32),
            pltpu.VMEM(tokens.shape, f32),
            dma((Z,)), dma, dma, dma, dma((Z,)), dma, dma((Z,)),
        ],
        compiler_params=pltpu.CompilerParams(
            collective_id=0, has_side_effects=True, vmem_limit_bytes=67_043_328
        ),
    )(tokens, out_grad, routes, routes.T, gates, gates.T, w_gate[0], w_up[0], w_down[0])
    return (mixed, token_grad, gate_grad, w_gate_grad[None], w_up_grad[None], w_down_grad[None])


def solution(mesh):
    by_token = P(("expert", "context", "dp"), None)
    by_expert = P(("expert", "context"), "dp", None)
    return jax.shard_map(
        shards,
        mesh=mesh,
        in_specs=(by_token,) * 4 + (by_expert,) * 3,
        out_specs=(by_token,) * 3 + (by_expert,) * 3,
        check_vma=False,
    )
```
